256 devices in a mesh: expert: 64 (over y, x, z_lo), dp: 4 (over z_hi, core).
Axes of the slice: x: 4, y: 4, z: 8 (z_hi: 2, z_lo: 4; z = z_hi * 4 + z_lo), core: 2. Of those that a mesh axis runs over, the one named last changes fastest.
Arguments:
- tokens: bfloat16 [3072, 3584], P('expert'), may hold values from -6 to 6
- expert_weights: bfloat16 [64, 3, 3584, 1024], P('expert', None, None, 'dp'), may hold values from -0.09375 to 0.09375
- partner: int32 [64], replicated, may hold values from 0 to 63, as said below
- replica: int32 [64], replicated, may hold values from 0 to 63, as said below
- routing: int32 [3072, 8], P('expert'), may hold values from 0 to 127, all different within a row; in each aligned block of 48 rows (0 to 47, 48 to 95, ...) at most 6 rows name the same one
- gates: bfloat16 [3072, 8], P('expert'), may hold values from 0.099609375 to 1
Outputs:
- mixed: bfloat16 [3072, 3584], P('expert', 'dp')
The draws below stay inside these ranges and needn't reach their ends.
Inputs may be any that keep to these rules, and one draw needn't show every extreme that they name: partner pairs devices: partner[partner[p]] = p; about half of the indices are paired with another, the rest with themselves. No expert appears more than 4 times in replica, and some expert appears exactly 4 times. `routing`: each row names 8 different slots; among the 48 rows of one device along expert no slot is named more than 6 times.
All inputs are finite; a program needn't handle non-finite values.
Results may differ from the reference program's by a relative error of at most 0.0058.
Values may be sent and summed in bfloat16 or wider, within the bound.
A program may use at most 128 MiB of HBM per device.

```python
import math
import jax
import jax.numpy as jnp
import numpy as np
from jax import lax

D = 3584
FF = 1024
TOPK = 8
RMAX = 4
TOK_DEV = 48
EXPERTS = 64
SLOTS = 128
CAP = 6
TOKENS = 3072
N_DP = 4


def draw_partner(key, part):
    shuffled = jax.random.permutation(jax.random.fold_in(key, 11), EXPERTS)
    position = jnp.arange(EXPERTS, dtype=jnp.int32)
    partner_slot = jnp.where(position < EXPERTS // 2, jnp.bitwise_xor(position, 1), position)
    inverse = jnp.argsort(shuffled, stable=True)
    return shuffled[partner_slot[inverse]].astype(jnp.int32)


def place_value(order, target, index):
    where_now = jnp.argmax((order == target).astype(jnp.int32)).astype(jnp.int32)
    moved = order[index]
    order = order.at[where_now].set(moved)
    return order.at[index].set(target).astype(jnp.int32)


def draw_replica(key, part):
    key_sizes = jax.random.fold_in(key, 21)
    key_experts = jax.random.fold_in(key, 22)
    key_order = jax.random.fold_in(key, 23)
    group_sizes = jax.random.randint(key_sizes, (EXPERTS,), 1, RMAX + 1).astype(jnp.int32)
    group_sizes = group_sizes.at[0].set(RMAX).at[1].set(1)
    group_starts = jnp.cumsum(group_sizes) - group_sizes
    position = jnp.arange(EXPERTS, dtype=jnp.int32)
    group_index = jnp.sum((group_starts[None, :] <= position[:, None]).astype(jnp.int32), axis=1) - 1
    expert_order = jax.random.permutation(key_experts, EXPERTS).astype(jnp.int32)
    expert_order = place_value(expert_order, EXPERTS - 1, 1)
    expert_order = place_value(expert_order, 0, 2)
    chosen = expert_order[group_index]
    reorder = jax.random.permutation(key_order, EXPERTS)
    return chosen[reorder].astype(jnp.int32)


def levels(stream_key, shape, pieces, smallest, high):
    level, own = 1.0, jax.random.fold_in(stream_key, 6)
    for axis_at, parts in pieces:
        draws = jnp.exp(jax.random.uniform(jax.random.fold_in(own, axis_at), (parts,), jnp.float32, smallest / len(pieces), high / len(pieces)))
        level = level * jnp.repeat(draws, shape[axis_at] // parts).reshape([-1 if axis == axis_at else 1 for axis in range(len(shape))])
    return level


def shared_out(key, own, number, rows, amount, top, bound, skew):
    order = jax.random.permutation(key, amount)
    crowded, common = shares(amount, rows * top, bound, skew, True), shares(amount, rows * top, bound, skew, False)
    places = jnp.arange(amount)

    def named(sizes, rotation):
        used = int((sizes > 0).sum())
        fixed = max(1, used // 4)
        moved = fixed + (places - fixed + rotation * (used - fixed)) % max(1, amount - fixed)
        return jnp.zeros((amount,), jnp.int32).at[order[jnp.where(places < fixed, places, moved)]].set(jnp.asarray(sizes, jnp.int32))

    sizes = jnp.where(number % 4 == 0, named(crowded, number // 4), named(common, number - number // 4 - 1))
    mixed = jax.random.permutation(jax.random.fold_in(own, 3), amount)
    giver, receiver = mixed[0:amount // 2 * 2:2], mixed[1:amount // 2 * 2:2]
    slack = jnp.minimum(sizes[giver] - 1, bound - sizes[receiver]) // 2
    slack = jnp.where((giver == order[0]) | (receiver == order[0]) | (sizes[receiver] == 0), 0, jnp.maximum(slack, 0))
    moved = jax.random.randint(jax.random.fold_in(own, 4), (amount // 2,), 0, 1 << 20) % (slack + 1)
    sizes = sizes.at[giver].add(-moved).at[receiver].add(moved)
    items = jnp.searchsorted(jnp.cumsum(sizes), jnp.arange(rows * top), side="right").astype(jnp.int32)
    listing = items.reshape(top, rows).T
    listing = listing[jax.random.permutation(jax.random.fold_in(own, 1), rows)]
    rotation = jax.random.randint(jax.random.fold_in(own, 2), (rows, 1), 0, top)
    return jnp.take_along_axis(listing, (jnp.arange(top)[None, :] + rotation) % top, axis=1)


def shares(count, total, reach, skew, full):
    portions = [(1 << 20) // math.isqrt(grade ** skew) + 1 for grade in range(1, count + 1)]
    largest = reach if full else min(reach, max(-(-total // count), total * portions[0] // sum(portions)))
    least = 1 if total - largest >= count - 1 else 0
    holding, rest = [largest] + [least] * (count - 1), total - largest - least * (count - 1)
    while rest > 0:
        movable = [i for i in range(1, count) if holding[i] < largest] or [i for i in range(1, count) if holding[i] < reach]
        whole, left = sum([portions[i] for i in movable]), rest
        for i in movable:
            extra = min(reach - holding[i], max(1, left * portions[i] // whole), rest)
            holding[i] = holding[i] + extra
            rest = rest - extra
    return np.array(holding)


def noise(rng, dims, width, most, cuts=(), kind=jnp.bfloat16):
    entries = width * jax.random.normal(rng, dims, jnp.float32)
    if cuts:
        entries = entries * levels(rng, dims, cuts, -0.22, 0.18)
    return jnp.clip(entries, -most, most).astype(kind)


def setup_inputs(seed: int = 0) -> dict:
    splits = jax.random.split(jax.random.key(seed), 7)
    tokens = noise(splits[0], (TOKENS, D), 1.0, 6.0, ((0, 64),))
    expert_weights = noise(splits[1], (EXPERTS, 3, D, FF), D ** -0.5, 0.09375, ((0, 64), (3, 4)))
    partner = draw_partner(jax.random.fold_in(splits[6], 71), 0)
    replica = draw_replica(jax.random.fold_in(splits[6], 71), 0)
    routing_keys = jax.random.split(jax.random.fold_in(splits[4], 1), TOKENS // TOK_DEV)
    routing_turns = jax.random.permutation(jax.random.fold_in(splits[4], 3), TOKENS // TOK_DEV)
    routing = jax.vmap(lambda own, number: shared_out(jax.random.fold_in(splits[4], 2), own, number, TOK_DEV, SLOTS, TOPK, CAP, 2))(routing_keys, routing_turns).reshape((TOKENS, TOPK))
    gates = jnp.clip(0.099609375 + 0.9003906 * jax.random.uniform(splits[5], (TOKENS, TOPK), jnp.float32) ** levels(splits[5], (TOKENS, TOPK), ((0, 64),), -0.2, 0.2), 0.099609375, 1.0).astype(jnp.bfloat16)
    return {"tokens": tokens, "expert_weights": expert_weights, "partner": partner, "replica": replica, "routing": routing, "gates": gates}


def reference(tokens, expert_weights, partner, replica, routing, gates):
    block_rows = 256
    pair_count = TOKENS * TOPK
    slot_table = jnp.stack([partner, replica], axis=1).reshape(-1).astype(jnp.int32)
    pair_expert = slot_table[routing.reshape(-1).astype(jnp.int32)].astype(jnp.int32)
    pair_token = (jnp.arange(pair_count, dtype=jnp.int32) // TOPK).astype(jnp.int32)
    pair_gate = gates.reshape(-1).astype(jnp.float32)
    counts = jnp.sum((pair_expert[:, None] == jnp.arange(EXPERTS, dtype=jnp.int32)[None, :]).astype(jnp.int32), axis=0)
    padded = ((counts + block_rows - 1) // block_rows) * block_rows
    starts = (jnp.cumsum(padded) - padded).astype(jnp.int32)
    firsts = (jnp.cumsum(counts) - counts).astype(jnp.int32)
    ordering = jnp.argsort(pair_expert, stable=True).astype(jnp.int32)
    sorted_expert = pair_expert[ordering]
    ranking = jnp.arange(pair_count, dtype=jnp.int32) - firsts[sorted_expert]
    destination = (starts[sorted_expert] + ranking).astype(jnp.int32)
    total_rows = pair_count + EXPERTS * block_rows
    row_token = jnp.zeros((total_rows,), jnp.int32).at[destination].set(pair_token[ordering])
    row_gate = jnp.zeros((total_rows,), jnp.float32).at[destination].set(pair_gate[ordering])
    block_start = jnp.arange(total_rows // block_rows, dtype=jnp.int32) * block_rows
    block_ends = starts + padded
    block_expert = jnp.minimum(jnp.sum((block_ends[None, :] <= block_start[:, None]).astype(jnp.int32), axis=1), EXPERTS - 1).astype(jnp.int32)
    quarter = FF // N_DP

    def run_block(operands):
        token_ids, gate_values, expert_id = operands
        rows_in = tokens[token_ids]
        weights = expert_weights[expert_id]
        gate_act = jnp.dot(rows_in, weights[0], preferred_element_type=jnp.float32)
        up_act = jnp.dot(rows_in, weights[1], preferred_element_type=jnp.float32)
        hidden = (jax.nn.silu(gate_act) * up_act).astype(jnp.bfloat16)
        total = jnp.zeros((block_rows, D), jnp.float32)
        for quarter_index in range(N_DP):
            lower_unit = quarter_index * quarter
            piece = jnp.dot(hidden[:, lower_unit:lower_unit + quarter], weights[2][:, lower_unit:lower_unit + quarter].T, preferred_element_type=jnp.float32)
            rounded = lax.optimization_barrier(piece.astype(jnp.bfloat16))
            total = total + rounded.astype(jnp.float32)
        return total * gate_values[:, None]

    contributions = lax.map(run_block, (row_token.reshape(-1, block_rows), row_gate.reshape(-1, block_rows), block_expert))
    mixed = jax.ops.segment_sum(contributions.reshape(-1, D), row_token, num_segments=TOKENS)
    return mixed.astype(jnp.bfloat16)
```

```python
import jax
import jax.numpy as jnp
from jax import lax
from jax.sharding import Mesh, PartitionSpec as P

GATHER_AXES = ("z_lo", "y", "x")
OWNER = ("y", "x", "z_lo")


def expert_hidden(packed, features, topk, hit, w):
    x = packed[:, :features]
    slots = packed[:, features:features + topk].astype(jnp.float32)
    weight = packed[:, features + topk:features + 2 * topk].astype(jnp.float32)
    ids = jnp.arange(hit.shape[0], dtype=jnp.float32)
    sel = jnp.sum(jnp.where((slots[:, :, None] == ids) & hit, weight[:, :, None], 0.0), axis=(1, 2))
    g = jnp.dot(x, w[0], preferred_element_type=jnp.float32)
    u = jnp.dot(x, w[1], preferred_element_type=jnp.float32)
    return (jax.nn.silu(g) * u).astype(jnp.bfloat16), sel


def down_project(h, sel, w_down):
    down = lax.dot_general(h, w_down, (((1,), (1,)), ((), ())), preferred_element_type=jnp.float32)
    return down * sel[:, None]


def shards(tokens, expert_weights, partner, replica, routing, gates):
    rows, features = tokens.shape
    topk = routing.shape[1]
    me = lax.axis_index(OWNER)
    core = lax.axis_index("core")
    half = rows // 2
    packed = jnp.concatenate(
        [tokens, routing.astype(jnp.bfloat16), gates, jnp.zeros((rows, 128 - 2 * topk), jnp.bfloat16)], axis=1
    )
    own = lax.dynamic_slice_in_dim(packed, core * half, half, axis=0)
    for axis in GATHER_AXES:
        own = lax.all_gather(own, axis, axis=0, tiled=True)
    other = lax.ppermute(own, "core", [(0, 1), (1, 0)])
    hit = jnp.stack([partner, replica], axis=1).reshape(-1) == me
    w = expert_weights[0]
    h_own, sel_own = expert_hidden(own, features, topk, hit, w)
    h_other, sel_other = expert_hidden(other, features, topk, hit, w)
    away = down_project(h_other, sel_other, w[2]).astype(jnp.bfloat16)
    returned = lax.ppermute(away, "core", [(0, 1), (1, 0)])
    total = (down_project(h_own, sel_own, w[2]) + returned.astype(jnp.float32)).astype(jnp.bfloat16)
    for axis in GATHER_AXES[::-1]:
        total = lax.psum_scatter(total, axis, scatter_dimension=0, tiled=True)
    total = lax.psum_scatter(total.astype(jnp.float32), "z_hi", scatter_dimension=1, tiled=True)
    return lax.all_to_all(total.astype(jnp.bfloat16), "core", split_axis=1, concat_axis=0, tiled=True)


def solution(mesh):
    grid = Mesh(mesh.devices.reshape(4, 4, 4, 2, 2), ("y", "x", "z_lo", "z_hi", "core"))
    dp = ("z_hi", "core")
    return jax.shard_map(
        shards,
        mesh=grid,
        in_specs=(
            P(OWNER, None),
            P(OWNER, None, None, dp),
            P(),
            P(),
            P(OWNER, None),
            P(OWNER, None),
        ),
        out_specs=P(OWNER, dp),
        check_vma=False,
    )
```

```python
import jax
import jax.numpy as jnp
import numpy as np
from jax import lax
from jax.sharding import Mesh, PartitionSpec as P

SIDE = 4
OWNER = ("y", "x", "z_lo")
EVERY = ("y", "x", "z_lo", "z_hi", "core")
IDS = np.arange(256).reshape(4, 4, 4, 2, 2)


def axis_rings(along):
    rings = []
    for core in range(2):
        moved = np.moveaxis(IDS[..., core], along[core], -1)
        rings += moved.reshape(-1, SIDE).tolist()
    return rings


SMALL = axis_rings((0, 1))
LARGE = axis_rings((1, 0))


def from_ahead(value, step):
    return lax.ppermute(value, EVERY, [(ring[(i + step) % SIDE], ring[i]) for ring in SMALL for i in range(SIDE)])


def from_behind(value, step):
    return lax.ppermute(value, EVERY, [(ring[i], ring[(i + step) % SIDE]) for ring in SMALL for i in range(SIDE)])


def expert_hidden(packed, features, topk, me, w):
    x = packed[:, :features]
    chosen = packed[:, features:features + topk].astype(jnp.float32)
    weight = packed[:, features + topk:features + 2 * topk].astype(jnp.float32)
    sel = jnp.sum(jnp.where(chosen == me.astype(jnp.float32), weight, 0.0), axis=1)
    g = jnp.dot(x, w[0], preferred_element_type=jnp.float32)
    u = jnp.dot(x, w[1], preferred_element_type=jnp.float32)
    return (jax.nn.silu(g) * u).astype(jnp.bfloat16), sel


def down_project(h, sel, w_down):
    down = lax.dot_general(h, w_down, (((1,), (1,)), ((), ())), preferred_element_type=jnp.float32)
    return down * sel[:, None]


def shards(tokens, expert_weights, partner, replica, routing, gates):
    rows, features = tokens.shape
    topk = routing.shape[1]
    me = lax.axis_index(OWNER)
    core = lax.axis_index("core")
    z_hi = lax.axis_index("z_hi")
    half = rows // 2
    slot_table = jnp.stack([partner, replica], axis=1).reshape(-1)
    named = routing[:, :, None] == jnp.arange(slot_table.shape[0], dtype=jnp.int32)
    chosen = jnp.sum(jnp.where(named, slot_table, 0), axis=2).astype(jnp.bfloat16)
    packed = jnp.concatenate(
        [tokens, chosen, gates, jnp.zeros((rows, 128 - 2 * topk), jnp.bfloat16)], axis=1
    )
    own = lax.dynamic_slice_in_dim(packed, core * half, half, axis=0)
    own = jnp.concatenate(
        [own] + [lax.ppermute(own, "z_lo", [((i + s) % SIDE, i) for i in range(SIDE)]) for s in range(1, SIDE)]
    )
    own = jnp.concatenate([own] + [from_ahead(own, s) for s in range(1, SIDE)])
    own = lax.all_gather(own, EVERY, axis=0, tiled=True, axis_index_groups=LARGE)
    other = lax.ppermute(own, "core", [(0, 1), (1, 0)])
    w = expert_weights[0]
    h_own, sel_own = expert_hidden(own, features, topk, me, w)
    h_other, sel_other = expert_hidden(other, features, topk, me, w)
    away = down_project(h_other, sel_other, w[2]).astype(jnp.bfloat16)
    returned = lax.ppermute(away, "core", [(0, 1), (1, 0)])
    total = (down_project(h_own, sel_own, w[2]) + returned.astype(jnp.float32)).astype(jnp.bfloat16)
    total = lax.psum_scatter(total, EVERY, scatter_dimension=0, tiled=True, axis_index_groups=LARGE)

    parts = total.reshape(SIDE, SIDE * half, features)
    total = parts[0].astype(jnp.float32)
    for s in range(1, SIDE):
        total = total + from_behind(parts[s], s).astype(jnp.float32)
    parts = total.astype(jnp.bfloat16).reshape(SIDE, half, features)
    total = total[:half]
    for s in range(1, SIDE):
        arrived = lax.ppermute(parts[s], "z_lo", [(i, (i + s) % SIDE) for i in range(SIDE)])
        total = total + arrived.astype(jnp.float32)
    wide = features // 2
    sent = lax.dynamic_slice_in_dim(total, (1 - z_hi) * wide, wide, axis=1).astype(jnp.bfloat16)
    arrived = lax.ppermute(sent, "z_hi", [(0, 1), (1, 0)])
    total = lax.dynamic_slice_in_dim(total, z_hi * wide, wide, axis=1) + arrived.astype(jnp.float32)
    return lax.all_to_all(total.astype(jnp.bfloat16), "core", split_axis=1, concat_axis=0, tiled=True)


def solution(mesh):
    grid = Mesh(mesh.devices.reshape(4, 4, 4, 2, 2), EVERY)
    dp = ("z_hi", "core")
    return jax.shard_map(
        shards,
        mesh=grid,
        in_specs=(
            P(OWNER, None),
            P(OWNER, None, None, dp),
            P(),
            P(),
            P(OWNER, None),
            P(OWNER, None),
        ),
        out_specs=P(OWNER, dp),
        check_vma=False,
    )
```

```python
import jax
import jax.numpy as jnp
import numpy as np
from jax import lax
from jax.sharding import Mesh, PartitionSpec as P

SIDE = 4
OWNER = ("y", "x", "z_lo")
EVERY = ("y", "x", "z_lo", "z_hi", "core")
IDS = np.arange(256).reshape(4, 4, 4, 2, 2)


def axis_rings(along):
    rings = []
    for core in range(2):
        moved = np.moveaxis(IDS[..., core], along[core], -1)
        rings += moved.reshape(-1, SIDE).tolist()
    return rings


SMALL = axis_rings((0, 1))
LARGE = axis_rings((1, 0))


def from_ahead(value, step):
    return lax.ppermute(value, EVERY, [(ring[(i + step) % SIDE], ring[i]) for ring in SMALL for i in range(SIDE)])


def from_behind(value, step):
    return lax.ppermute(value, EVERY, [(ring[i], ring[(i + step) % SIDE]) for ring in SMALL for i in range(SIDE)])


def expert_hidden(packed, features, topk, me, w):
    x = packed[:, :features]
    chosen = packed[:, features:features + topk].astype(jnp.float32)
    weight = packed[:, features + topk:features + 2 * topk].astype(jnp.float32)
    sel = jnp.sum(jnp.where(chosen == me.astype(jnp.float32), weight, 0.0), axis=1)
    g = jnp.dot(x, w[0], preferred_element_type=jnp.float32)
    u = jnp.dot(x, w[1], preferred_element_type=jnp.float32)
    return (jax.nn.silu(g) * u).astype(jnp.bfloat16), sel


def down_project(h, sel, w_down):
    down = lax.dot_general(h, w_down, (((1,), (1,)), ((), ())), preferred_element_type=jnp.float32)
    return down * sel[:, None]


def shards(tokens, expert_weights, partner, replica, routing, gates):
    rows, features = tokens.shape
    topk = routing.shape[1]
    me = lax.axis_index(OWNER)
    core = lax.axis_index("core")
    z_hi = lax.axis_index("z_hi")
    half = rows // 2
    slot_table = jnp.stack([partner, replica], axis=1).reshape(-1)
    named = routing[:, :, None] == jnp.arange(slot_table.shape[0], dtype=jnp.int32)
    chosen = jnp.sum(jnp.where(named, slot_table, 0), axis=2).astype(jnp.bfloat16)
    packed = jnp.concatenate(
        [tokens, chosen, gates, jnp.zeros((rows, 128 - 2 * topk), jnp.bfloat16)], axis=1
    )
    own = lax.dynamic_slice_in_dim(packed, core * half, half, axis=0)
    own = jnp.concatenate(
        [own] + [lax.ppermute(own, "z_lo", [((i + s) % SIDE, i) for i in range(SIDE)]) for s in range(1, SIDE)]
    )
    near = jnp.concatenate([own, from_ahead(own, 1)])
    far = jnp.concatenate([from_ahead(own, 2), from_ahead(own, 3)])
    w = expert_weights[0]
    first = lax.all_gather(near, EVERY, axis=0, tiled=True, axis_index_groups=LARGE)
    first, far = lax.optimization_barrier((first, far))
    second = lax.all_gather(far, EVERY, axis=0, tiled=True, axis_index_groups=LARGE)
    parts = []
    for turn in range(2):
        mine = first if turn == 0 else second
        other = lax.ppermute(mine, "core", [(0, 1), (1, 0)])
        h_other, sel_other = expert_hidden(other, features, topk, me, w)
        away = down_project(h_other, sel_other, w[2]).astype(jnp.bfloat16)
        returned = lax.ppermute(away, "core", [(0, 1), (1, 0)])
        h_own, sel_own = expert_hidden(mine, features, topk, me, w)
        total = (down_project(h_own, sel_own, w[2]) + returned.astype(jnp.float32)).astype(jnp.bfloat16)
        if turn == 0:
            total, second = lax.optimization_barrier((total, second))
        total = lax.psum_scatter(total, EVERY, scatter_dimension=0, tiled=True, axis_index_groups=LARGE)
        parts += [total[:SIDE * half], total[SIDE * half:]]

    total = parts[0].astype(jnp.float32)
    for s in range(1, SIDE):
        total = total + from_behind(parts[s], s).astype(jnp.float32)
    parts = total.astype(jnp.bfloat16).reshape(SIDE, half, features)
    total = total[:half]
    for s in range(1, SIDE):
        arrived = lax.ppermute(parts[s], "z_lo", [(i, (i + s) % SIDE) for i in range(SIDE)])
        total = total + arrived.astype(jnp.float32)
    wide = features // 2
    sent = lax.dynamic_slice_in_dim(total, (1 - z_hi) * wide, wide, axis=1).astype(jnp.bfloat16)
    arrived = lax.ppermute(sent, "z_hi", [(0, 1), (1, 0)])
    total = lax.dynamic_slice_in_dim(total, z_hi * wide, wide, axis=1) + arrived.astype(jnp.float32)
    return lax.all_to_all(total.astype(jnp.bfloat16), "core", split_axis=1, concat_axis=0, tiled=True)


def solution(mesh):
    grid = Mesh(mesh.devices.reshape(4, 4, 4, 2, 2), EVERY)
    dp = ("z_hi", "core")
    return jax.shard_map(
        shards,
        mesh=grid,
        in_specs=(
            P(OWNER, None),
            P(OWNER, None, None, dp),
            P(),
            P(),
            P(OWNER, None),
            P(OWNER, None),
        ),
        out_specs=P(OWNER, dp),
        check_vma=False,
    )
```

```python
import jax
import jax.numpy as jnp
import numpy as np
from jax import lax
from jax.sharding import Mesh, PartitionSpec as P

SIDE = 4
OWNER = ("y", "x", "z_lo")
EVERY = ("y", "x", "z_lo", "z_hi", "core")
IDS = np.arange(256).reshape(4, 4, 4, 2, 2)


def axis_rings(along):
    rings = []
    for core in range(2):
        moved = np.moveaxis(IDS[..., core], along[core], -1)
        rings += moved.reshape(-1, SIDE).tolist()
    return rings


SMALL = axis_rings((0, 1))
LARGE = axis_rings((1, 0))


def from_ahead(value, step):
    return lax.ppermute(value, EVERY, [(ring[(i + step) % SIDE], ring[i]) for ring in SMALL for i in range(SIDE)])


def from_behind(value, step):
    return lax.ppermute(value, EVERY, [(ring[i], ring[(i + step) % SIDE]) for ring in SMALL for i in range(SIDE)])


def expert_hidden(packed, features, topk, me, w):
    x = packed[:, :features]
    chosen = packed[:, features:features + topk].astype(jnp.float32)
    weight = packed[:, features + topk:features + 2 * topk].astype(jnp.float32)
    sel = jnp.sum(jnp.where(chosen == me.astype(jnp.float32), weight, 0.0), axis=1)
    g = jnp.dot(x, w[0], preferred_element_type=jnp.float32)
    u = jnp.dot(x, w[1], preferred_element_type=jnp.float32)
    return (jax.nn.silu(g) * u).astype(jnp.bfloat16), sel


def down_project(h, sel, w_down):
    down = lax.dot_general(h, w_down, (((1,), (1,)), ((), ())), preferred_element_type=jnp.float32)
    return down * sel[:, None]


def shards(tokens, expert_weights, partner, replica, routing, gates):
    rows, features = tokens.shape
    topk = routing.shape[1]
    me = lax.axis_index(OWNER)
    core = lax.axis_index("core")
    z_hi = lax.axis_index("z_hi")
    half = rows // 2
    slot_table = jnp.stack([partner, replica], axis=1).reshape(-1)
    named = routing[:, :, None] == jnp.arange(slot_table.shape[0], dtype=jnp.int32)
    chosen = jnp.sum(jnp.where(named, slot_table, 0), axis=2).astype(jnp.bfloat16)
    packed = jnp.concatenate(
        [tokens, chosen, gates, jnp.zeros((rows, 128 - 2 * topk), jnp.bfloat16)], axis=1
    )
    own = lax.dynamic_slice_in_dim(packed, core * half, half, axis=0)
    own = jnp.concatenate(
        [own] + [lax.ppermute(own, "z_lo", [((i + s) % SIDE, i) for i in range(SIDE)]) for s in range(1, SIDE)]
    )
    near = jnp.concatenate([own, from_ahead(own, 1)])
    far = jnp.concatenate([from_ahead(own, 2), from_ahead(own, 3)])
    w = expert_weights[0]
    first = lax.all_gather(near, EVERY, axis=0, tiled=True, axis_index_groups=LARGE)
    first, far = lax.optimization_barrier((first, far))
    second = lax.all_gather(far, EVERY, axis=0, tiled=True, axis_index_groups=LARGE)
    parts = []
    for turn in range(2):
        mine = first if turn == 0 else second
        other = lax.ppermute(mine, "core", [(0, 1), (1, 0)])
        h_other, sel_other = expert_hidden(other, features, topk, me, w)
        away = down_project(h_other, sel_other, w[2]).astype(jnp.bfloat16)
        returned = lax.ppermute(away, "core", [(0, 1), (1, 0)])
        h_own, sel_own = expert_hidden(mine, features, topk, me, w)
        total = (down_project(h_own, sel_own, w[2]) + returned.astype(jnp.float32)).astype(jnp.bfloat16)
        if turn == 0:
            total, second = lax.optimization_barrier((total, second))
        total = lax.psum_scatter(total, EVERY, scatter_dimension=0, tiled=True, axis_index_groups=LARGE)
        parts += [total[:SIDE * half], total[SIDE * half:]]

    total = parts[0].astype(jnp.float32)
    for s in range(1, SIDE):
        total = total + from_behind(parts[s], s).astype(jnp.float32)
    wide = features // 2
    here = lax.dynamic_slice_in_dim(total, z_hi * wide, wide, axis=1)
    there = lax.dynamic_slice_in_dim(total, (1 - z_hi) * wide, wide, axis=1)
    total = here[:half]
    for s in range(SIDE):
        for flip, source in ((0, here), (1, there)):
            if s or flip:
                sent = source[s * half:(s + 1) * half].astype(jnp.bfloat16)
                route = [(2 * i + j, 2 * ((i + s) % SIDE) + (j ^ flip)) for i in range(SIDE) for j in range(2)]
                total = total + lax.ppermute(sent, ("z_lo", "z_hi"), route).astype(jnp.float32)
    return lax.all_to_all(total.astype(jnp.bfloat16), "core", split_axis=1, concat_axis=0, tiled=True)


def solution(mesh):
    grid = Mesh(mesh.devices.reshape(4, 4, 4, 2, 2), EVERY)
    dp = ("z_hi", "core")
    return jax.shard_map(
        shards,
        mesh=grid,
        in_specs=(
            P(OWNER, None),
            P(OWNER, None, None, dp),
            P(),
            P(),
            P(OWNER, None),
            P(OWNER, None),
        ),
        out_specs=P(OWNER, dp),
        check_vma=False,
    )
```
